256 devices in a mesh: cuts: 8 (over x, core), rows: 32 (over y, z).
Axes of the slice: x: 4, y: 4, z: 8, core: 2. Of those that a mesh axis runs over, the one named last changes fastest.
Arguments:
- start_states: bfloat16 [32768, 1024], P('rows', 'cuts'), may hold values from -6 to 6
- diag_blocks: bfloat16 [256, 128, 128], P('rows'), may hold values from -0.25 to 0.25
- local_blocks: bfloat16 [512, 128, 128], P('rows'), may hold values from -0.1875 to 0.1875
- local_first: int32 [512], P('rows'), may hold values from 0 to 7
- local_second: int32 [512], P('rows'), may hold values from 0 to 7
- far_blocks: bfloat16 [1024, 128, 128], P('rows'), may hold values from -0.1875 to 0.1875
- far_home: int32 [1024], P('rows'), may hold values from 0 to 7
- far_device: int32 [1024, 1], P('rows'), may hold values from 0 to 31; in each aligned block of 32 rows (0 to 31, 32 to 63, ...) at most 2 rows name the same one
- far_cluster: int32 [1024], P('rows'), may hold values from 0 to 7
- bounds: float32 [8, 2], P('cuts'), may hold values from -1.3 to 3.5, as said below
Outputs:
- subspace: float32 [32768, 1024], P('rows', 'cuts')
- rayleigh: float32 [1024, 128], P('cuts')
The draws below stay inside these ranges and needn't reach their ends.
Inputs may be any that keep to these rules, and one draw needn't show every extreme that they name: `far_device`: among the 32 far pairs of one index of rows, no index of rows is named more than 2 times, a bound that some block reaches. `bounds`: row s holds slice s's lower bound in column 0, between -1.3 and -0.5, and its upper bound in column 1, between 2.5 and 3.5.
All inputs are finite; a program needn't handle non-finite values.
Results may differ from the reference program's by a relative error of at most 0.009.
Values may be sent and summed in bfloat16 or wider, within the bound.
No kernel may reach another device: no remote copies, remote signals or barrier semaphores. Data moves between devices by JAX's collectives and lax.ppermute only.
A program may use at most 64 MiB of HBM per device.

```python
import math
import jax
import jax.numpy as jnp
import numpy as np
from jax import lax

BS = 128
M = 128
CL_DEV = 8
LOC_DEV = 16
CAP = 2
FAR_DEV = 32
DEGREE = 2
SLICES = 8
NCL = 256
NB = 32768
LOC_TOTAL = 512
FAR_TOTAL = 1024
WIDE = 1024
N_ROWS = 32


def draw_bounds(key, part):
    first_key, second_key = jax.random.split(jax.random.fold_in(key, 17))
    lows = jax.random.uniform(first_key, (SLICES,), jnp.float32, -1.3, -0.5)
    highs = jax.random.uniform(second_key, (SLICES,), jnp.float32, 2.5, 3.5)
    return jnp.stack([lows, highs], axis=1)


def touch_ends(array, stream_key, least, largest):
    longest = array.shape.index(max(array.shape))
    spots = []
    for shift in (0, 1):
        where = [jax.random.randint(jax.random.fold_in(stream_key, axis), (), 0, length) for axis, length in enumerate(array.shape)]
        where[longest] = (where[longest] + shift) % array.shape[longest]
        spots.append(tuple(where))
    return array.at[spots[0]].set(least).at[spots[1]].set(largest)


def steps_of(key, dims, shards, low, top_value):
    level, own = 1.0, jax.random.fold_in(key, 6)
    for axis_at, blocks in shards:
        heights = jnp.exp(jax.random.uniform(jax.random.fold_in(own, axis_at), (blocks,), jnp.float32, low / len(shards), top_value / len(shards)))
        level = level * jnp.repeat(heights, dims[axis_at] // blocks).reshape([-1 if axis == axis_at else 1 for axis in range(len(dims))])
    return level


def shared_out(own_key, own, number, rows, count, top, limit, slope):
    ranking = jax.random.permutation(own_key, count)
    packed, common = load_shares(count, rows * top, limit, slope, True), load_shares(count, rows * top, limit, slope, False)
    places = jnp.arange(count)

    def named(tallies, rotation):
        used = int((tallies > 0).sum())
        fixed = max(1, used // 4)
        moved = fixed + (places - fixed + rotation * (used - fixed)) % max(1, count - fixed)
        return jnp.zeros((count,), jnp.int32).at[ranking[jnp.where(places < fixed, places, moved)]].set(jnp.asarray(tallies, jnp.int32))

    tallies = jnp.where(number % 4 == 0, named(packed, number // 4), named(common, number - number // 4 - 1))
    mixed = jax.random.permutation(jax.random.fold_in(own, 3), count)
    donor, receiver = mixed[0:count // 2 * 2:2], mixed[1:count // 2 * 2:2]
    margin = jnp.minimum(tallies[donor] - 1, limit - tallies[receiver]) // 2
    margin = jnp.where((donor == ranking[0]) | (receiver == ranking[0]) | (tallies[receiver] == 0), 0, jnp.maximum(margin, 0))
    moved = jax.random.randint(jax.random.fold_in(own, 4), (count // 2,), 0, 1 << 20) % (margin + 1)
    tallies = tallies.at[donor].add(-moved).at[receiver].add(moved)
    labels = jnp.searchsorted(jnp.cumsum(tallies), jnp.arange(rows * top), side="right").astype(jnp.int32)
    table = labels.reshape(top, rows).T
    table = table[jax.random.permutation(jax.random.fold_in(own, 1), rows)]
    rotation = jax.random.randint(jax.random.fold_in(own, 2), (rows, 1), 0, top)
    return jnp.take_along_axis(table, (jnp.arange(top)[None, :] + rotation) % top, axis=1)


def load_shares(number_of, total, most, lean, full):
    weights = [(1 << 20) // math.isqrt(standing ** lean) + 1 for standing in range(1, number_of + 1)]
    largest = most if full else min(most, max(-(-total // number_of), total * weights[0] // sum(weights)))
    least = 1 if total - largest >= number_of - 1 else 0
    holding, surplus = [largest] + [least] * (number_of - 1), total - largest - least * (number_of - 1)
    while surplus > 0:
        candidates = [i for i in range(1, number_of) if holding[i] < largest] or [i for i in range(1, number_of) if holding[i] < most]
        pool, budget = sum([weights[i] for i in candidates]), surplus
        for i in candidates:
            extra = min(most - holding[i], max(1, budget * weights[i] // pool), surplus)
            holding[i] = holding[i] + extra
            surplus = surplus - extra
    return np.array(holding)


def centred(stream_key, extent, deviation, limit, shards=(), kind=jnp.bfloat16):
    loudness = steps_of(stream_key, extent, shards, -0.22, 0.18) if shards else 1.0
    array = jax.random.normal(stream_key, extent, jnp.float32) * deviation * loudness
    return jnp.minimum(jnp.maximum(array, -limit), limit).astype(kind)


def setup_inputs(seed: int = 0) -> dict:
    splits = jax.random.split(jax.random.key(seed), 11)
    start_states = centred(splits[0], (NB, WIDE), 1.0, 6.0, ((0, 32), (1, 8)))
    diag_blocks = centred(splits[1], (NCL, BS, BS), (4 * BS) ** -0.5, 0.25, ((0, 32),))
    local_blocks = centred(splits[2], (LOC_TOTAL, BS, BS), (8 * BS) ** -0.5, 0.1875, ((0, 32),))
    local_first = touch_ends(jax.random.randint(splits[3], (LOC_TOTAL,), 0, CL_DEV), jax.random.fold_in(splits[3], 1), 0, CL_DEV - 1).astype(jnp.int32)
    local_second = touch_ends(jax.random.randint(splits[4], (LOC_TOTAL,), 0, CL_DEV), jax.random.fold_in(splits[4], 1), 0, CL_DEV - 1).astype(jnp.int32)
    far_blocks = centred(splits[5], (FAR_TOTAL, BS, BS), (8 * BS) ** -0.5, 0.1875, ((0, 32),))
    far_home = touch_ends(jax.random.randint(splits[6], (FAR_TOTAL,), 0, CL_DEV), jax.random.fold_in(splits[6], 1), 0, CL_DEV - 1).astype(jnp.int32)
    far_device_keys = jax.random.split(jax.random.fold_in(splits[7], 1), FAR_TOTAL // FAR_DEV)
    far_device_turns = jax.random.permutation(jax.random.fold_in(splits[7], 3), FAR_TOTAL // FAR_DEV)
    far_device = jax.vmap(lambda own, number: shared_out(jax.random.fold_in(splits[7], 2), own, number, FAR_DEV, N_ROWS, 1, CAP, 2))(far_device_keys, far_device_turns).reshape((FAR_TOTAL, 1))
    far_cluster = touch_ends(jax.random.randint(splits[8], (FAR_TOTAL,), 0, CL_DEV), jax.random.fold_in(splits[8], 1), 0, CL_DEV - 1).astype(jnp.int32)
    bounds = draw_bounds(jax.random.fold_in(splits[10], 71), 0)
    return {"start_states": start_states, "diag_blocks": diag_blocks, "local_blocks": local_blocks, "local_first": local_first, "local_second": local_second, "far_blocks": far_blocks, "far_home": far_home, "far_device": far_device, "far_cluster": far_cluster, "bounds": bounds}


def symmetric_blocks(raw_blocks):
    widened = raw_blocks.astype(jnp.float32)
    return (0.5 * (widened + jnp.swapaxes(widened, 1, 2))).astype(jnp.bfloat16)

def round_trip(values):
    narrow = lax.optimization_barrier(values.astype(jnp.bfloat16))
    return narrow.astype(jnp.float32)

def apply_operator(rounded, symmetric, local_blocks, local_first, local_second, far_blocks, far_home, far_device, far_cluster):
    count = rounded.shape[0]
    columns = rounded.shape[2]
    widened = rounded.astype(jnp.float32)
    result = jnp.einsum('cab,cbw->caw', symmetric.astype(jnp.float32), widened)
    per_row = widened.reshape(N_ROWS, CL_DEV, BS, columns)

    def local_part(inputs):
        blocks, first_index, second_index, own_rows = inputs
        wide_blocks = blocks.astype(jnp.float32)
        forward = jnp.einsum('pab,pbw->paw', wide_blocks, own_rows[second_index])
        backward = jnp.einsum('pba,pbw->paw', wide_blocks, own_rows[first_index])
        empty = jnp.zeros((CL_DEV, BS, columns), jnp.float32)
        return empty.at[first_index].add(forward).at[second_index].add(backward)
    local_sum = lax.map(local_part, (local_blocks.reshape(N_ROWS, LOC_DEV, BS, BS), local_first.reshape(N_ROWS, LOC_DEV), local_second.reshape(N_ROWS, LOC_DEV), per_row))
    result = result + local_sum.reshape(count, BS, columns)
    owners = jnp.arange(N_ROWS, dtype=jnp.int32)[:, None] * CL_DEV
    homes = owners + far_home.reshape(N_ROWS, FAR_DEV)
    others = far_device.reshape(N_ROWS, FAR_DEV) * CL_DEV + far_cluster.reshape(N_ROWS, FAR_DEV)

    def far_step(running, inputs):
        blocks, home_index, other_index = inputs
        wide_blocks = blocks.astype(jnp.float32)
        toward_home = round_trip(jnp.einsum('pab,pbw->paw', wide_blocks, widened[other_index]))
        toward_far = round_trip(jnp.einsum('pba,pbw->paw', wide_blocks, widened[home_index]))
        running = running.at[home_index].add(toward_home).at[other_index].add(toward_far)
        return (running, None)
    result, _ = lax.scan(far_step, result, (far_blocks.reshape(N_ROWS, FAR_DEV, BS, BS), homes, others))
    return result

def orthonormal(block_field, gram_matrix, total_rows):
    lower_factor = jnp.linalg.cholesky(gram_matrix / total_rows)
    identity = jnp.eye(M, dtype=jnp.float32)
    inverse = jax.vmap(lambda matrix: jax.scipy.linalg.solve_triangular(matrix, identity, lower=True))(lower_factor)
    return jnp.einsum('rsm,snm->rsn', block_field, inverse, precision=lax.Precision.HIGHEST)

def reference(start_states, diag_blocks, local_blocks, local_first, local_second, far_blocks, far_home, far_device, far_cluster, bounds):
    symmetric = symmetric_blocks(diag_blocks)
    total_rows = start_states.shape[0]
    count = total_rows // BS
    slice_count = bounds.shape[0]
    center = (0.5 * (bounds[:, 1] + bounds[:, 0]))[:, None]
    half_width = (0.5 * (bounds[:, 1] - bounds[:, 0]))[:, None]
    highest = lax.Precision.HIGHEST

    def operate(start_field):
        rounded = start_field.astype(jnp.bfloat16).reshape(count, BS, slice_count * M)
        result = apply_operator(rounded, symmetric, local_blocks, local_first, local_second, far_blocks, far_home, far_device[:, 0], far_cluster)
        return result.reshape(total_rows, slice_count, M)

    def filtered(start_field):
        applied = operate(start_field)
        previous = start_field
        current = (applied - center * start_field) / half_width
        for degree_step in range(1, DEGREE):
            following = 2.0 * (operate(current) - center * current) / half_width - previous
            previous, current = (current, following)
        return (current, applied)
    first_field = start_states.astype(jnp.float32).reshape(total_rows, slice_count, M)
    first_filtered, _ = filtered(first_field)
    first_gram = jnp.einsum('rsm,rsn->smn', first_filtered, first_filtered, precision=highest)
    basis_one = orthonormal(first_filtered, first_gram, total_rows)
    second_filtered, applied = filtered(basis_one)
    rayleigh = jnp.einsum('rsm,rsn->smn', basis_one, applied, precision=highest) / total_rows
    lower_basis = jnp.concatenate([jnp.zeros((total_rows, 1, M), jnp.float32), basis_one[:, :-1]], axis=1)
    projection = jnp.einsum('rsm,rsn->smn', lower_basis, second_filtered, precision=highest)
    deflated = second_filtered - jnp.einsum('rsm,smn->rsn', lower_basis, projection, precision=highest) / total_rows
    second_gram = jnp.einsum('rsm,rsn->smn', deflated, deflated, precision=highest)
    subspace = orthonormal(deflated, second_gram, total_rows)
    return (subspace.reshape(total_rows, slice_count * M), rayleigh.reshape(slice_count * M, M))
```

```python
import jax
import jax.numpy as jnp
import numpy as np
from jax import lax
from jax.experimental import pallas as pl
from jax.experimental.pallas import tpu as pltpu
from jax.sharding import Mesh
from jax.sharding import PartitionSpec as P

CAP = 2

NX, NC, NY, NZ = 4, 2, 4, 8
PER = 11
ROWS = PER * 128 + 16
HIGH = lax.Precision.HIGHEST


def shifted(value, axis, distance):
    size = lax.axis_size(axis)
    return lax.ppermute(value, axis, [(i, (i + distance) % size) for i in range(size)])


def crossing(k, back):
    pairs = []
    for x in range(NX):
        for z in range(NZ):
            half = (z % 2) ^ k
            there = (z // 2) * NZ + 2 * x + half
            pairs.append((there, x * NZ + z) if back else (x * NZ + z, there))
    return pairs


def crossed(first, second, odd, back):
    send = (jnp.where(odd, second, first), jnp.where(odd, first, second))
    got = [lax.ppermute(send[k], ("x", "z"), crossing(k, back)) for k in (0, 1)]
    return jnp.where(odd, got[1], got[0]), jnp.where(odd, got[0], got[1])


def product_kernel(tab, pa, pb, f0, x1, x2, x3, y1, y2, y3, own, ox1, ox2, ox3, oy1, oy2, oy3, fld, acc):
    for k, ref in enumerate((f0, x1, x2, x3, y1, y2, y3)):
        fld[16 * k : 16 * (k + 1)] = ref[...]
    acc[...] = jnp.zeros_like(acc)
    for part, ref in enumerate((pa, pb)):
        base = part * NZ * 2 * PER

        def step(q, carry, ref=ref, base=base):
            for b in range(PER):
                block = ref[q, b * 128 : (b + 1) * 128, :]
                home = tab[base + q * 2 * PER + b]
                far = tab[base + q * 2 * PER + PER + b]
                toward_home = lax.dot_general(
                    fld[far], block, (((1,), (1,)), ((), ())), preferred_element_type=jnp.float32
                )
                if b < PER - 1:
                    toward_far = lax.dot_general(
                        fld[home], block, (((1,), (0,)), ((), ())), preferred_element_type=jnp.float32
                    )
                acc[home] += toward_home
                if b < PER - 1:
                    acc[far] += toward_far
            return carry

        lax.fori_loop(0, NZ, step, 0)
    own[...] = acc[0:16]
    for k, ref in enumerate((ox1, ox2, ox3, oy1, oy2, oy3)):
        ref[...] = acc[16 * (k + 1) : 16 * (k + 2)].astype(jnp.bfloat16)


def products(tab, pa, pb, fields):
    cols = fields[0].shape[1]
    shape = (16, cols, 128)
    vmem = pl.BlockSpec(memory_space=pltpu.VMEM)
    return pl.pallas_call(
        product_kernel,
        out_shape=[jax.ShapeDtypeStruct(shape, jnp.float32)] + [jax.ShapeDtypeStruct(shape, jnp.bfloat16)] * 6,
        in_specs=[pl.BlockSpec(memory_space=pltpu.SMEM)] + [vmem] * 9,
        out_specs=[vmem] * 7,
        scratch_shapes=[
            pltpu.VMEM((112, cols, 128), jnp.bfloat16),
            pltpu.VMEM((112, cols, 128), jnp.float32),
        ],
        compiler_params=pltpu.CompilerParams(vmem_limit_bytes=40 << 20),
        cost_estimate=pl.CostEstimate(flops=336 * 2 * 64 * 128 * 128, bytes_accessed=8 << 20, transcendentals=0),
        name="products",
    )(tab, pa, pb, *fields)


def own_payload(diag_blocks, local_blocks, local_first, local_second, far_blocks, far_home, far_device, far_cluster):
    x, c, y, z = (lax.axis_index(a) for a in ("x", "core", "y", "z"))
    target = far_device[:, 0]
    to_y, to_z = target // NZ, target % NZ
    pairs = far_blocks.shape[0]
    number = jnp.arange(pairs, dtype=jnp.int32)
    before = jnp.sum(
        ((target[None, :] == target[:, None]) & (number[None, :] < number[:, None])).astype(jnp.int32), axis=1
    )
    slot = (to_y % 2) * 4 + (to_z % 2) * CAP + before
    mine = (to_z // 2 == x) & (to_y // 2 == c)
    chosen = (slot[None, :] == jnp.arange(8, dtype=jnp.int32)[:, None]) & mine[None, :]
    taken = chosen.astype(jnp.int32)
    home_base = ((x - z // 2) % NX) * 16 + (z % 2) * 8
    away = (y - to_y) % NY
    far_index = jnp.where(away == 0, 0, 3 + away) * 16 + (to_z % 2) * 8 + far_cluster
    far_h = home_base + jnp.sum(taken * far_home[None, :], axis=1)
    far_f = jnp.sum(taken * far_index[None, :], axis=1)
    far_part = jnp.einsum(
        "sp,pab->sab", chosen.astype(jnp.bfloat16), far_blocks, preferred_element_type=jnp.float32
    ).astype(jnp.bfloat16)
    at = 4 * x + 2 * c
    local_part = lax.dynamic_slice_in_dim(local_blocks, at, 2, 0)
    loc_h = home_base + lax.dynamic_slice_in_dim(local_first, at, 2, 0)
    loc_f = home_base + lax.dynamic_slice_in_dim(local_second, at, 2, 0)
    raw = lax.dynamic_slice_in_dim(diag_blocks, 2 * x + c, 1, 0).astype(jnp.float32)
    diag_part = (0.5 * (raw + jnp.swapaxes(raw, 1, 2))).astype(jnp.bfloat16)
    dia = (home_base + 2 * x + c)[None]
    homes = jnp.concatenate([far_h, loc_h, dia])
    fars = jnp.concatenate([far_f, loc_f, dia])
    table = jnp.pad(jnp.stack([homes, fars]), ((0, 14), (0, 128 - PER))).astype(jnp.bfloat16)
    blocks = jnp.concatenate([far_part, local_part, diag_part]).reshape(PER * 128, 128)
    return jnp.concatenate([blocks, table])


def spread(payload):
    up = down = payload
    got = [payload]
    for _ in range(3):
        up = shifted(up, "z", 1)
        down = shifted(down, "z", -1)
        got += [up, down]
    cut = 704
    got.append(jnp.concatenate([shifted(up[:cut], "z", 1), shifted(down[cut:], "z", -1)]))
    mine = jnp.stack(got)
    other = lax.ppermute(mine, "core", [(0, 1), (1, 0)])
    return mine, other


def table_of(payload):
    return payload[:, PER * 128 : PER * 128 + 2, :PER].astype(jnp.int32).reshape(-1)


def total(parts, axes):
    rows = parts.shape[0]
    peers = NY * NZ
    pieces = parts.reshape(peers, rows // peers, 128)
    mine = jnp.sum(lax.all_to_all(pieces, axes, 0, 0, tiled=True), axis=0)
    return lax.all_to_all(
        jnp.broadcast_to(mine[None], (peers, *mine.shape)), axes, 0, 0, tiled=True
    ).reshape(rows, 128)


def mm(a, b):
    return jnp.dot(a, b, precision=HIGH)


def gram(a, b):
    return jnp.einsum("cma,cna->mn", a, b, preferred_element_type=jnp.float32)


def inverse_factor(matrix):
    factor = jnp.linalg.cholesky(matrix)
    return jax.scipy.linalg.solve_triangular(factor, jnp.eye(128, dtype=jnp.float32), lower=True)


def body(
    start_states,
    diag_blocks,
    local_blocks,
    local_first,
    local_second,
    far_blocks,
    far_home,
    far_device,
    far_cluster,
    bounds,
):
    z = lax.axis_index("z")
    odd = z % 2 == 1
    count = 1024.0 * NY * NZ
    turned = jnp.swapaxes(start_states.reshape(8, 128, 128), 1, 2).reshape(8, 2, 64, 128)
    field = jnp.concatenate(crossed(turned[:, 0], turned[:, 1], odd, False))
    limits = lax.ppermute(bounds, ("x", "z"), crossing(0, False))
    center = 0.5 * (limits[0, 1] + limits[0, 0])
    half_width = 0.5 * (limits[0, 1] - limits[0, 0])
    payload = own_payload(
        diag_blocks, local_blocks, local_first, local_second, far_blocks, far_home, far_device, far_cluster
    )
    pa, pb = spread(payload)
    tab = jnp.concatenate([table_of(pa), table_of(pb)])

    def operate(rounded):
        fields = [rounded]
        fields += [shifted(rounded, "x", k) for k in (1, 2, 3)]
        fields += [shifted(rounded, "y", k) for k in (1, 2, 3)]
        own, *sums = products(tab, pa, pb, fields)
        for k in (1, 2, 3):
            own = own + shifted(sums[k - 1], "x", -k).astype(jnp.float32)
            own = own + shifted(sums[k + 2], "y", -k).astype(jnp.float32)
        return own

    def filtered(start):
        applied = operate(start.astype(jnp.bfloat16))
        current = (applied - center * start) / half_width
        following = 2.0 * (operate(current.astype(jnp.bfloat16)) - center * current) / half_width - start
        return following, applied

    def rows_of(value):
        value = value.astype(jnp.bfloat16)
        halves = crossed(value[:8], value[8:], odd, True)
        return jnp.concatenate(halves, axis=1)

    first, _ = filtered(field.astype(jnp.float32))
    second, applied = filtered(first)
    y_rows = rows_of(first)
    w_rows = rows_of(applied)
    y_low = lax.ppermute(
        y_rows, ("x", "core"), [(i, i + 1) for i in range(NX * NC - 1)]
    )
    early = total(jnp.concatenate([gram(y_rows, y_rows), gram(y_rows, w_rows)]), ("y", "z"))
    a1 = inverse_factor(early[:128] / count)
    a_low = lax.ppermute(a1, ("x", "core"), [(i, i + 1) for i in range(NX * NC - 1)])
    rayleigh = mm(mm(a1, early[128:]), a1.T) / count
    v_rows = rows_of(second)
    late = total(jnp.concatenate([gram(v_rows, v_rows), gram(y_low, v_rows)]), ("y", "z"))
    projection = mm(mm(a_low, late[128:]), a1.T)
    deflated = mm(mm(a1, late[:128]), a1.T) - mm(projection.T, projection) / count
    a2 = inverse_factor(deflated / count)
    keep = mm(a2, a1)
    drop = mm(a2, mm(projection.T, a_low)) / count
    subspace = jnp.einsum("cja,kj->cak", v_rows.astype(jnp.float32), keep, precision=HIGH) - jnp.einsum(
        "cja,kj->cak", y_low.astype(jnp.float32), drop, precision=HIGH
    )
    return subspace.reshape(1024, 128), rayleigh


def solution(mesh):
    grid = Mesh(np.asarray(mesh.devices).reshape(NX, NC, NY, NZ), ("x", "core", "y", "z"))
    rows, cuts = ("y", "z"), ("x", "core")
    placed = (
        P(rows, cuts),
        P(rows, None, None),
        P(rows, None, None),
        P(rows),
        P(rows),
        P(rows, None, None),
        P(rows),
        P(rows, None),
        P(rows),
        P(cuts, None),
    )
    return jax.shard_map(
        body, mesh=grid, in_specs=placed, out_specs=(P(rows, cuts), P(cuts, None)), check_vma=False
    )
```

```python
import functools

import jax
import jax.numpy as jnp
import numpy as np
from jax import lax
from jax.experimental import pallas as pl
from jax.experimental.pallas import tpu as pltpu
from jax.sharding import Mesh
from jax.sharding import PartitionSpec as P

CAP = 2

NX, NC, NY, NZ = 4, 2, 4, 8
PER = 11
ROWS = PER * 128 + 16
HIGH = lax.Precision.HIGHEST


def shifted(value, axis, distance):
    size = lax.axis_size(axis)
    return lax.ppermute(value, axis, [(i, (i + distance) % size) for i in range(size)])


def crossing(k, back):
    pairs = []
    for x in range(NX):
        for z in range(NZ):
            half = (z % 2) ^ k
            there = (z // 2) * NZ + 2 * x + half
            pairs.append((there, x * NZ + z) if back else (x * NZ + z, there))
    return pairs


def crossed(first, second, odd, back):
    send = (jnp.where(odd, second, first), jnp.where(odd, first, second))
    got = [lax.ppermute(send[k], ("x", "z"), crossing(k, back)) for k in (0, 1)]
    return jnp.where(odd, got[1], got[0]), jnp.where(odd, got[0], got[1])


def product_kernel(tab, pa, pb, f0, x1, x2, x3, y1, y2, y3, own, ox1, ox2, ox3, oy1, oy2, oy3, fld, acc):
    for k, ref in enumerate((f0, x1, x2, x3, y1, y2, y3)):
        fld[16 * k : 16 * (k + 1)] = ref[...]
    acc[...] = jnp.zeros_like(acc)
    for part, ref in enumerate((pa, pb)):
        base = part * NZ * 2 * PER

        def step(q, carry, ref=ref, base=base):
            for b in range(PER):
                block = ref[q, b * 128 : (b + 1) * 128, :]
                home = tab[base + q * 2 * PER + b]
                far = tab[base + q * 2 * PER + PER + b]
                toward_home = lax.dot_general(
                    fld[far], block, (((1,), (1,)), ((), ())), preferred_element_type=jnp.float32
                )
                if b < PER - 1:
                    toward_far = lax.dot_general(
                        fld[home], block, (((1,), (0,)), ((), ())), preferred_element_type=jnp.float32
                    )
                acc[home] += toward_home
                if b < PER - 1:
                    acc[far] += toward_far
            return carry

        lax.fori_loop(0, NZ, step, 0)
    own[...] = acc[0:16]
    for k, ref in enumerate((ox1, ox2, ox3, oy1, oy2, oy3)):
        ref[...] = acc[16 * (k + 1) : 16 * (k + 2)].astype(jnp.bfloat16)


def products(tab, pa, pb, fields):
    cols = fields[0].shape[1]
    shape = (16, cols, 128)
    vmem = pl.BlockSpec(memory_space=pltpu.VMEM)
    return pl.pallas_call(
        product_kernel,
        out_shape=[jax.ShapeDtypeStruct(shape, jnp.float32)] + [jax.ShapeDtypeStruct(shape, jnp.bfloat16)] * 6,
        in_specs=[pl.BlockSpec(memory_space=pltpu.SMEM)] + [vmem] * 9,
        out_specs=[vmem] * 7,
        scratch_shapes=[
            pltpu.VMEM((112, cols, 128), jnp.bfloat16),
            pltpu.VMEM((112, cols, 128), jnp.float32),
        ],
        compiler_params=pltpu.CompilerParams(vmem_limit_bytes=40 << 20),
        cost_estimate=pl.CostEstimate(flops=336 * 2 * 64 * 128 * 128, bytes_accessed=8 << 20, transcendentals=0),
        name="products",
    )(tab, pa, pb, *fields)


def own_payload(diag_blocks, local_blocks, local_first, local_second, far_blocks, far_home, far_device, far_cluster):
    x, c, y, z = (lax.axis_index(a) for a in ("x", "core", "y", "z"))
    target = far_device[:, 0]
    to_y, to_z = target // NZ, target % NZ
    pairs = far_blocks.shape[0]
    number = jnp.arange(pairs, dtype=jnp.int32)
    before = jnp.sum(
        ((target[None, :] == target[:, None]) & (number[None, :] < number[:, None])).astype(jnp.int32), axis=1
    )
    slot = (to_y % 2) * 4 + (to_z % 2) * CAP + before
    mine = (to_z // 2 == x) & (to_y // 2 == c)
    chosen = (slot[None, :] == jnp.arange(8, dtype=jnp.int32)[:, None]) & mine[None, :]
    taken = chosen.astype(jnp.int32)
    home_base = ((x - z // 2) % NX) * 16 + (z % 2) * 8
    away = (y - to_y) % NY
    far_index = jnp.where(away == 0, 0, 3 + away) * 16 + (to_z % 2) * 8 + far_cluster
    far_h = home_base + jnp.sum(taken * far_home[None, :], axis=1)
    far_f = jnp.sum(taken * far_index[None, :], axis=1)
    far_part = jnp.einsum(
        "sp,pab->sab", chosen.astype(jnp.bfloat16), far_blocks, preferred_element_type=jnp.float32
    ).astype(jnp.bfloat16)
    at = 4 * x + 2 * c
    local_part = lax.dynamic_slice_in_dim(local_blocks, at, 2, 0)
    loc_h = home_base + lax.dynamic_slice_in_dim(local_first, at, 2, 0)
    loc_f = home_base + lax.dynamic_slice_in_dim(local_second, at, 2, 0)
    raw = lax.dynamic_slice_in_dim(diag_blocks, 2 * x + c, 1, 0).astype(jnp.float32)
    diag_part = (0.5 * (raw + jnp.swapaxes(raw, 1, 2))).astype(jnp.bfloat16)
    dia = (home_base + 2 * x + c)[None]
    homes = jnp.concatenate([far_h, loc_h, dia])
    fars = jnp.concatenate([far_f, loc_f, dia])
    table = jnp.pad(jnp.stack([homes, fars]), ((0, 14), (0, 128 - PER))).astype(jnp.bfloat16)
    blocks = jnp.concatenate([far_part, local_part, diag_part]).reshape(PER * 128, 128)
    return jnp.concatenate([blocks, table])


def spread(payload, fields):
    up = down = payload
    got = [payload]
    for n in range(3):
        up = shifted(up, "z", 1)
        down = shifted(down, "z", -1)
        got += [up, down]
        if n == 1:
            up, down, *fields = lax.optimization_barrier((up, down, *fields))
    cut = 704
    got.append(jnp.concatenate([shifted(up[:cut], "z", 1), shifted(down[cut:], "z", -1)]))
    mine = jnp.stack(got)
    other = lax.ppermute(mine, "core", [(0, 1), (1, 0)])
    return mine, other, fields


def table_of(payload):
    return payload[:, PER * 128 : PER * 128 + 2, :PER].astype(jnp.int32).reshape(-1)


def summed(value, axis, masks, kind):
    sent = value.astype(kind)
    got = [
        lax.ppermute(sent, axis, [(i, i ^ m) for i in range(lax.axis_size(axis))]).astype(jnp.float32)
        for m in masks
    ]
    mine = sent.astype(jnp.float32)
    if len(masks) == 1:
        return mine + got[0]
    return (mine + got[0]) + (got[1] + got[2])


def total(value, kind):
    value = summed(value, "z", (1, 2, 3), kind)
    value = summed(value, "y", (1, 2, 3), kind)
    return summed(value, "z", (4,), jnp.float32)


def mm(a, b, contract=(1, 0)):
    dims = (((contract[0],), (contract[1],)), ((), ()))
    return lax.dot_general(a, b, dims, precision=HIGH, preferred_element_type=jnp.float32)


def inverse_factor(gram, sref, eref):
    row = lax.broadcasted_iota(jnp.int32, (128, 128), 0)
    col = lax.broadcasted_iota(jnp.int32, (128, 128), 1)
    eye = jnp.where(row == col, 1.0, 0.0).astype(jnp.float32)
    half_low = jnp.where(row > col, 1.0, 0.5 * eye)
    down = lax.rsqrt(jnp.sum(gram * eye, axis=1, keepdims=True))
    along = lax.rsqrt(jnp.sum(gram * eye, axis=0, keepdims=True))
    state = gram * down * along
    eref[...] = eye * down
    for _ in range(4):
        step = eye - half_low * (state - eye)
        eref[...] = mm(step, eref[...])
        state = mm(mm(step, state), step, (1, 1))
    inverse = eref[...]
    state = mm(mm(inverse, gram), inverse, (1, 1))
    eref[...] = mm(eye - half_low * (state - eye), inverse)
    close = jnp.max(jnp.abs(state - eye)) < 1e-3

    @pl.when(jnp.logical_not(close))
    def _():
        sref[...] = gram
        eref[...] = eye

        def step(k, carry):
            value = sref[...]
            top = sref[pl.ds(k, 1), :]
            pivot = jnp.sum(jnp.where(col[:1] == k, top, 0.0), axis=1, keepdims=True)
            left = jnp.sum(jnp.where(col == k, value, 0.0), axis=1, keepdims=True)
            scale = jnp.where(row[:, :1] > k, left / pivot, 0.0)
            below = eref[...] - scale * eref[pl.ds(k, 1), :]
            sref[...] = value - scale * top
            eref[...] = below
            return carry

        lax.fori_loop(0, 128, step, 0)
        eref[...] = eref[...] * lax.rsqrt(jnp.sum(sref[...] * eye, axis=1, keepdims=True))

    return eref[...]


def joined(low, high, c):
    return jnp.concatenate([low[c], high[c]], axis=0)


def inner(a, b):
    return lax.dot_general(a, b, (((1,), (1,)), ((), ())), preferred_element_type=jnp.float32)


def vmem_call(kernel, shapes, scratch, name, *args):
    vmem = pl.BlockSpec(memory_space=pltpu.VMEM)
    many = isinstance(shapes, list)
    return pl.pallas_call(
        kernel,
        out_shape=shapes,
        in_specs=[vmem] * len(args),
        out_specs=[vmem] * len(shapes) if many else vmem,
        scratch_shapes=scratch,
        cost_estimate=pl.CostEstimate(flops=1 << 28, bytes_accessed=1 << 20, transcendentals=0),
        name=name,
    )(*args)


SQUARE = jax.ShapeDtypeStruct((128, 128), jnp.float32)
PAIR = [pltpu.VMEM((128, 128), jnp.float32)] * 2


def first_gram_kernel(y0, y1, out):
    total_gram = jnp.zeros((128, 128), jnp.float32)
    for c in range(8):
        y = joined(y0, y1, c)
        total_gram += inner(y, y)
    out[...] = total_gram


def factor_kernel(count, gram, out, sref, eref):
    out[...] = inverse_factor(gram[...] * (1.0 / count), sref, eref)


def grams_kernel(v0, v1, w0, w1, y0, y1, low, out):
    vv = lv = yw = jnp.zeros((128, 128), jnp.float32)
    for c in range(8):
        v = joined(v0, v1, c)
        vv += inner(v, v)
        lv += inner(low[c], v)
        yw += inner(joined(y0, y1, c), joined(w0, w1, c))
    out[0:128] = vv
    out[128:256] = lv
    out[256:384] = yw


def in_two(value):
    high = value.astype(jnp.bfloat16)
    return high, (value - high.astype(jnp.float32)).astype(jnp.bfloat16)


def finish_kernel(count, sums, a1_ref, a_low_ref, v0, v1, low, subspace, rayleigh, sref, eref):
    a1 = a1_ref[...]
    a_low = a_low_ref[...]
    part = 1.0 / count
    projection = mm(mm(a_low, sums[128:256]), a1, (1, 1))
    whole = mm(mm(a1, sums[0:128]), a1, (1, 1))
    deflated = whole - part * mm(projection, projection, (0, 0))
    a2 = inverse_factor(deflated * part, sref, eref)
    keep = in_two(mm(a1, a2, (0, 1)))
    drop = in_two(mm(a_low, mm(projection, a2, (1, 1)), (0, 0)) * (-part))
    for c in range(8):
        v = joined(v0, v1, c)
        rows = jnp.zeros((128, 128), jnp.float32)
        for left, rights in ((v, keep), (low[c], drop)):
            for right in rights:
                rows += lax.dot_general(
                    left, right, (((0,), (0,)), ((), ())), preferred_element_type=jnp.float32
                )
        subspace[c * 128 : (c + 1) * 128] = rows
    rayleigh[...] = mm(mm(a1, sums[256:384]), a1, (1, 1)) * part


def body(
    start_states,
    diag_blocks,
    local_blocks,
    local_first,
    local_second,
    far_blocks,
    far_home,
    far_device,
    far_cluster,
    bounds,
):
    z = lax.axis_index("z")
    odd = z % 2 == 1
    count = 1024.0 * NY * NZ
    turned = jnp.swapaxes(start_states.reshape(8, 128, 128), 1, 2).reshape(8, 2, 64, 128)
    field = jnp.concatenate(crossed(turned[:, 0], turned[:, 1], odd, False))
    limits = lax.ppermute(bounds, ("x", "z"), crossing(0, False))
    center = 0.5 * (limits[0, 1] + limits[0, 0])
    half_width = 0.5 * (limits[0, 1] - limits[0, 0])
    payload = own_payload(
        diag_blocks, local_blocks, local_first, local_second, far_blocks, far_home, far_device, far_cluster
    )
    def gathered(rounded):
        fields = [rounded]
        fields += [shifted(rounded, "x", k) for k in (1, 2, 3)]
        fields += [shifted(rounded, "y", k) for k in (1, 2, 3)]
        return fields

    payload, field = lax.optimization_barrier((payload, field))
    pa, pb, fields = spread(payload, gathered(field))
    tab = jnp.concatenate([table_of(pa), table_of(pb)])

    def operate(fields):
        own, *sums = products(tab, pa, pb, fields)
        for k in (1, 2, 3):
            own = own + shifted(sums[k - 1], "x", -k).astype(jnp.float32)
            own = own + shifted(sums[k + 2], "y", -k).astype(jnp.float32)
        return own

    def filtered(start, fields):
        applied = operate(fields)
        current = (applied - center * start) / half_width
        again = operate(gathered(current.astype(jnp.bfloat16)))
        following = 2.0 * (again - center * current) / half_width - start
        return following, applied

    def rows_of(value):
        value = value.astype(jnp.bfloat16)
        return crossed(value[:8], value[8:], odd, True)

    upward = [(i, i + 1) for i in range(NX * NC - 1)]
    first, _ = filtered(field.astype(jnp.float32), fields)
    second, applied = filtered(first, gathered(first.astype(jnp.bfloat16)))
    y0, y1 = rows_of(first)
    y_low = lax.ppermute(jnp.concatenate([y0, y1], axis=1), ("x", "core"), upward)
    gram = total(vmem_call(first_gram_kernel, SQUARE, [], "first_gram", y0, y1), jnp.float32)
    a1 = vmem_call(functools.partial(factor_kernel, count), SQUARE, PAIR, "factor", gram)
    a_low = lax.ppermute(a1, ("x", "core"), upward)
    w0, w1 = rows_of(applied)
    v0, v1 = rows_of(second)
    sums = total(
        vmem_call(
            grams_kernel,
            jax.ShapeDtypeStruct((384, 128), jnp.float32),
            [],
            "grams",
            v0, v1, w0, w1, y0, y1, y_low,
        ),
        jnp.bfloat16,
    )
    subspace, rayleigh = vmem_call(
        functools.partial(finish_kernel, count),
        [jax.ShapeDtypeStruct((1024, 128), jnp.float32), SQUARE],
        PAIR,
        "finish",
        sums, a1, a_low, v0, v1, y_low,
    )
    return subspace, rayleigh


def solution(mesh):
    grid = Mesh(np.asarray(mesh.devices).reshape(NX, NC, NY, NZ), ("x", "core", "y", "z"))
    rows, cuts = ("y", "z"), ("x", "core")
    placed = (
        P(rows, cuts),
        P(rows, None, None),
        P(rows, None, None),
        P(rows),
        P(rows),
        P(rows, None, None),
        P(rows),
        P(rows, None),
        P(rows),
        P(cuts, None),
    )
    return jax.shard_map(
        body, mesh=grid, in_specs=placed, out_specs=(P(rows, cuts), P(cuts, None)), check_vma=False
    )
```

```python
import functools

import jax
import jax.numpy as jnp
import numpy as np
from jax import lax
from jax.experimental import pallas as pl
from jax.experimental.pallas import tpu as pltpu
from jax.sharding import Mesh
from jax.sharding import PartitionSpec as P

CAP = 2

NX, NC, NY, NZ = 4, 2, 4, 8
PER = 11
HIGH = lax.Precision.HIGHEST


Z = ("zh", "zl")


def shifted(value, axis, distance):
    size = NZ if axis == Z else 4
    return lax.ppermute(value, axis, [(i, (i + distance) % size) for i in range(size)])


def crossing(k, back):
    pairs = []
    for x in range(NX):
        for z in range(NZ):
            half = (z % 2) ^ k
            there = (z // 2) * NZ + 2 * x + half
            pairs.append((there, x * NZ + z) if back else (x * NZ + z, there))
    return pairs


def crossed(first, second, odd, back):
    send = (jnp.where(odd, second, first), jnp.where(odd, first, second))
    got = [lax.ppermute(send[k], ("x", *Z), crossing(k, back)) for k in (0, 1)]
    return jnp.where(odd, got[1], got[0]), jnp.where(odd, got[0], got[1])


def product_kernel(tab, pa, pb, f0, x1, x2, x3, y1, y2, y3, own, ox1, ox2, ox3, oy1, oy2, oy3, fld, acc):
    for k, ref in enumerate((f0, x1, x2, x3, y1, y2, y3)):
        fld[16 * k : 16 * (k + 1)] = ref[...]
    acc[...] = jnp.zeros_like(acc)
    for part, ref in enumerate((pa, pb)):
        base = part * NZ * 2 * PER

        def step(q, carry, ref=ref, base=base):
            at = base + q * 2 * PER
            for first in range(0, PER, 2):
                places, terms = [], []
                for b in range(first, min(first + 2, PER)):
                    block = ref[q, b * 128 : (b + 1) * 128, :]
                    home = tab[at + b]
                    far = tab[at + PER + b]
                    places.append(home)
                    terms.append(
                        lax.dot_general(
                            fld[far], block, (((1,), (1,)), ((), ())), preferred_element_type=jnp.float32
                        )
                    )
                    if b < PER - 1:
                        places.append(far)
                        terms.append(
                            lax.dot_general(
                                fld[home], block, (((1,), (0,)), ((), ())), preferred_element_type=jnp.float32
                            )
                        )
                held = [acc[place] for place in places]
                for i, place in enumerate(places):
                    value = held[i]
                    for j in range(i):
                        value = jnp.where(places[j] == place, held[j], value)
                    held[i] = value + terms[i]
                for place, value in zip(places, held):
                    acc[place] = value
            return carry

        lax.fori_loop(0, NZ, step, 0)
    own[...] = acc[0:16]
    for k, ref in enumerate((ox1, ox2, ox3, oy1, oy2, oy3)):
        ref[...] = acc[16 * (k + 1) : 16 * (k + 2)].astype(jnp.bfloat16)


def products(tab, pa, pb, fields):
    cols = fields[0].shape[1]
    shape = (16, cols, 128)
    vmem = pl.BlockSpec(memory_space=pltpu.VMEM)
    return pl.pallas_call(
        product_kernel,
        out_shape=[jax.ShapeDtypeStruct(shape, jnp.float32)] + [jax.ShapeDtypeStruct(shape, jnp.bfloat16)] * 6,
        in_specs=[pl.BlockSpec(memory_space=pltpu.SMEM)] + [vmem] * 9,
        out_specs=[vmem] * 7,
        scratch_shapes=[
            pltpu.VMEM((112, cols, 128), jnp.bfloat16),
            pltpu.VMEM((112, cols, 128), jnp.float32),
        ],
        compiler_params=pltpu.CompilerParams(vmem_limit_bytes=40 << 20),
        cost_estimate=pl.CostEstimate(flops=336 * 2 * 64 * 128 * 128, bytes_accessed=8 << 20, transcendentals=0),
        name="products",
    )(tab, pa, pb, *fields)


def own_payload(diag_blocks, local_blocks, local_first, local_second, far_blocks, far_home, far_device, far_cluster):
    x, c, y, z = (lax.axis_index(a) for a in ("x", "core", "y", Z))
    target = far_device[:, 0]
    to_y, to_z = target // NZ, target % NZ
    pairs = far_blocks.shape[0]
    number = jnp.arange(pairs, dtype=jnp.int32)
    before = jnp.sum(
        ((target[None, :] == target[:, None]) & (number[None, :] < number[:, None])).astype(jnp.int32), axis=1
    )
    slot = (to_y % 2) * 4 + (to_z % 2) * CAP + before
    mine = (to_z // 2 == x) & (to_y // 2 == c)
    chosen = (slot[None, :] == jnp.arange(8, dtype=jnp.int32)[:, None]) & mine[None, :]
    taken = chosen.astype(jnp.int32)
    home_base = ((x - z // 2) % NX) * 16 + (z % 2) * 8
    away = (y - to_y) % NY
    far_index = jnp.where(away == 0, 0, 3 + away) * 16 + (to_z % 2) * 8 + far_cluster
    far_h = home_base + jnp.sum(taken * far_home[None, :], axis=1)
    far_f = jnp.sum(taken * far_index[None, :], axis=1)
    far_part = jnp.einsum(
        "sp,pab->sab", chosen.astype(jnp.bfloat16), far_blocks, preferred_element_type=jnp.float32
    ).astype(jnp.bfloat16)
    at = 4 * x + 2 * c
    local_part = lax.dynamic_slice_in_dim(local_blocks, at, 2, 0)
    loc_h = home_base + lax.dynamic_slice_in_dim(local_first, at, 2, 0)
    loc_f = home_base + lax.dynamic_slice_in_dim(local_second, at, 2, 0)
    raw = lax.dynamic_slice_in_dim(diag_blocks, 2 * x + c, 1, 0).astype(jnp.float32)
    diag_part = (0.5 * (raw + jnp.swapaxes(raw, 1, 2))).astype(jnp.bfloat16)
    dia = (home_base + 2 * x + c)[None]
    homes = jnp.concatenate([far_h, loc_h, dia])
    fars = jnp.concatenate([far_f, loc_f, dia])
    table = jnp.pad(jnp.stack([homes, fars]), ((0, 14), (0, 128 - PER))).astype(jnp.bfloat16)
    blocks = jnp.concatenate([far_part, local_part, diag_part]).reshape(PER * 128, 128)
    return jnp.concatenate([blocks, table])


def spread(payload, fields):
    up = down = payload
    got = [payload]
    for n in range(3):
        up = shifted(up, Z, 1)
        down = shifted(down, Z, -1)
        got += [up, down]
        if n == 1:
            up, down, *fields = lax.optimization_barrier((up, down, *fields))
    cut = 704
    got.append(jnp.concatenate([shifted(up[:cut], Z, 1), shifted(down[cut:], Z, -1)]))
    mine = jnp.stack(got)
    other = lax.ppermute(mine, "core", [(0, 1), (1, 0)])
    return mine, other, fields


def table_of(payload):
    return payload[:, PER * 128 : PER * 128 + 2, :PER].astype(jnp.int32).reshape(-1)


def share_of(value):
    pieces = value.reshape(NY * NZ, -1, 128)
    pieces = lax.all_to_all(pieces, ("y", "x", "zl"), 0, 0, tiled=True)
    return jnp.sum(pieces.astype(jnp.float32), axis=0)


def put_together(share):
    every = jnp.broadcast_to(share[None], (NY * NZ, *share.shape))
    return lax.all_to_all(every, ("y", *Z), 0, 0, tiled=True).reshape(-1, 128)


def mm(a, b, contract=(1, 0)):
    dims = (((contract[0],), (contract[1],)), ((), ()))
    return lax.dot_general(a, b, dims, precision=HIGH, preferred_element_type=jnp.float32)


def inverse_factors(grams, srefs, erefs):
    row = lax.broadcasted_iota(jnp.int32, (128, 128), 0)
    col = lax.broadcasted_iota(jnp.int32, (128, 128), 1)
    eye = jnp.where(row == col, 1.0, 0.0).astype(jnp.float32)
    half_low = jnp.where(row > col, 1.0, 0.5 * eye)
    inverses, states = [], []
    for gram in grams:
        down = lax.rsqrt(jnp.sum(gram * eye, axis=1, keepdims=True))
        along = lax.rsqrt(jnp.sum(gram * eye, axis=0, keepdims=True))
        inverses.append(eye * down)
        states.append(gram * down * along)
    for _ in range(4):
        steps = [eye - half_low * (state - eye) for state in states]
        inverses = [mm(step, inverse) for step, inverse in zip(steps, inverses)]
        states = [mm(step, state) for step, state in zip(steps, states)]
        states = [mm(state, step, (1, 1)) for step, state in zip(steps, states)]
    states = [mm(inverse, gram) for inverse, gram in zip(inverses, grams)]
    states = [mm(state, inverse, (1, 1)) for inverse, state in zip(inverses, states)]
    for gram, inverse, state, sref, eref in zip(grams, inverses, states, srefs, erefs):
        eref[...] = mm(eye - half_low * (state - eye), inverse)
        close = jnp.max(jnp.abs(state - eye)) < 1e-3

        @pl.when(jnp.logical_not(close))
        def _(gram=gram, sref=sref, eref=eref):
            sref[...] = gram
            eref[...] = eye

            def step(k, carry):
                value = sref[...]
                top = sref[pl.ds(k, 1), :]
                pivot = jnp.sum(jnp.where(col[:1] == k, top, 0.0), axis=1, keepdims=True)
                left = jnp.sum(jnp.where(col == k, value, 0.0), axis=1, keepdims=True)
                scale = jnp.where(row[:, :1] > k, left / pivot, 0.0)
                below = eref[...] - scale * eref[pl.ds(k, 1), :]
                sref[...] = value - scale * top
                eref[...] = below
                return carry

            lax.fori_loop(0, 128, step, 0)
            eref[...] = eref[...] * lax.rsqrt(jnp.sum(sref[...] * eye, axis=1, keepdims=True))

    return [eref[...] for eref in erefs]


def joined(low, high):
    return jnp.concatenate([low, high], axis=0)


def inner(a, b):
    return lax.dot_general(a, b, (((1,), (1,)), ((), ())), preferred_element_type=jnp.float32)


def grams_kernel(v, t, y, low, out):
    sums = [jnp.zeros((128, 128), jnp.float32)] * 5
    for c in range(8):
        vc, tc, yc, lc = (joined(ref[0, c], ref[1, c]) for ref in (v, t, y, low))
        for i, (left, right) in enumerate(((vc, vc), (lc, vc), (yc, tc), (yc, yc), (lc, lc))):
            sums[i] += inner(left, right)
    for i in range(5):
        out[128 * i : 128 * (i + 1)] = sums[i].astype(jnp.bfloat16)


def in_two(value):
    high = value.astype(jnp.bfloat16)
    return high, (value - high.astype(jnp.float32)).astype(jnp.bfloat16)


def finish_kernel(count, lead, limits, sums, v_ref, low, subspace, rayleigh, *refs):
    srefs, erefs = refs[:2], refs[2:]
    part = 1.0 / count
    vv, lv, yt, yy, ll = (sums[128 * i : 128 * (i + 1)] for i in range(5))
    row = lax.broadcasted_iota(jnp.int32, (128, 128), 0)
    col = lax.broadcasted_iota(jnp.int32, (128, 128), 1)
    ll = jnp.where(lead[0] == 1, jnp.where(row == col, count, 0.0), ll)
    a1, a_low = inverse_factors([yy * part, ll * part], srefs, erefs)
    projection = mm(mm(a_low, lv), a1, (1, 1))
    whole = mm(mm(a1, vv), a1, (1, 1))
    deflated = whole - part * mm(projection, projection, (0, 0))
    (a2,) = inverse_factors([deflated * part], srefs[:1], erefs[:1])
    keep = in_two(mm(a1, a2, (0, 1)))
    drop = in_two(mm(a_low, mm(projection, a2, (1, 1)), (0, 0)) * (-part))
    for c in range(8):
        rows = jnp.zeros((128, 128), jnp.float32)
        for source, rights in ((v_ref, keep), (low, drop)):
            left = joined(source[0, c], source[1, c])
            for right in rights:
                rows += lax.dot_general(
                    left, right, (((0,), (0,)), ((), ())), preferred_element_type=jnp.float32
                )
        subspace[c * 128 : (c + 1) * 128] = rows
    center = 0.5 * (limits[0, 1] + limits[0, 0])
    half_width = 0.5 * (limits[0, 1] - limits[0, 0])
    rayleigh[...] = mm(mm(a1, half_width * yt + center * yy), a1, (1, 1)) * part


def body(
    start_states,
    diag_blocks,
    local_blocks,
    local_first,
    local_second,
    far_blocks,
    far_home,
    far_device,
    far_cluster,
    bounds,
):
    z = lax.axis_index(Z)
    odd = z % 2 == 1
    count = 1024.0 * NY * NZ
    turned = jnp.swapaxes(start_states.reshape(8, 128, 128), 1, 2).reshape(8, 2, 64, 128)
    field = jnp.concatenate(crossed(turned[:, 0], turned[:, 1], odd, False))
    limits = lax.ppermute(bounds, ("x", *Z), crossing(0, False))
    center = 0.5 * (limits[0, 1] + limits[0, 0])
    half_width = 0.5 * (limits[0, 1] - limits[0, 0])
    payload = own_payload(
        diag_blocks, local_blocks, local_first, local_second, far_blocks, far_home, far_device, far_cluster
    )

    def gathered(rounded):
        fields = [rounded]
        fields += [shifted(rounded, "x", k) for k in (1, 2, 3)]
        fields += [shifted(rounded, "y", k) for k in (1, 2, 3)]
        return fields

    payload, field = lax.optimization_barrier((payload, field))
    pa, pb, fields = spread(payload, gathered(field))
    tab = jnp.concatenate([table_of(pa), table_of(pb)])

    def operate(fields):
        own, *sums = products(tab, pa, pb, fields)
        for k in (1, 2, 3):
            own = own + shifted(sums[k - 1], "x", -k).astype(jnp.float32)
            own = own + shifted(sums[k + 2], "y", -k).astype(jnp.float32)
        return own

    def filtered(start, fields):
        middle = (operate(fields) - center * start) / half_width
        return middle, gathered(middle.astype(jnp.bfloat16))

    def last(start, middle, fields):
        return 2.0 * (operate(fields) - center * middle) / half_width - start

    def paired(value):
        value = value.astype(jnp.bfloat16)
        low, high = value[:8], value[8:]
        got = lax.ppermute(jnp.where(odd, low, high), Z, [(i, i ^ 1) for i in range(NZ)])
        kept = jnp.where(odd, high, low)
        return jnp.stack([jnp.where(odd, got, kept), jnp.where(odd, kept, got)])

    def placed(value):
        return lax.ppermute(value, ("x", *Z), crossing(0, True))

    start = field.astype(jnp.float32)
    middle, fields = filtered(start, fields)
    first = last(start, middle, fields)
    fields = gathered(first.astype(jnp.bfloat16))
    y_rows, *fields = lax.optimization_barrier((paired(first), *fields))
    middle, fields = filtered(first, fields)
    below = [(z, NZ + z) for z in range(NZ)] + [(NZ + z, z + 2) for z in range(NZ - 2)]
    y_low = lax.ppermute(y_rows, ("core", *Z), below)
    t_rows, y_low, *fields = lax.optimization_barrier((paired(middle), y_low, *fields))
    y_placed = placed(y_low)
    second = last(first, middle, fields)
    v_rows = paired(second)
    v_placed = placed(v_rows)
    vmem = pl.BlockSpec(memory_space=pltpu.VMEM)
    smem = pl.BlockSpec(memory_space=pltpu.SMEM)
    sums = pl.pallas_call(
        grams_kernel,
        out_shape=jax.ShapeDtypeStruct((640, 128), jnp.bfloat16),
        in_specs=[vmem] * 4,
        out_specs=vmem,
        name="gram_sums",
    )(v_rows, t_rows, y_rows, y_low)
    share = placed(share_of(sums))
    sums = put_together(share)
    lead = ((lax.axis_index("x") == 0) & (lax.axis_index("core") == 0)).astype(jnp.int32)[None]
    subspace, rayleigh = pl.pallas_call(
        functools.partial(finish_kernel, count),
        out_shape=[jax.ShapeDtypeStruct((1024, 128), jnp.float32), jax.ShapeDtypeStruct((128, 128), jnp.float32)],
        in_specs=[smem, smem] + [vmem] * 3,
        out_specs=[vmem] * 2,
        scratch_shapes=[pltpu.VMEM((128, 128), jnp.float32)] * 4,
        name="finish",
    )(lead, bounds, sums, v_placed, y_placed)
    return subspace, rayleigh


def solution(mesh):
    grid = Mesh(np.asarray(mesh.devices).reshape(NX, NC, NY, NZ // 2, 2), ("x", "core", "y", *Z))
    rows, cuts = ("y", *Z), ("x", "core")
    placed = (
        P(rows, cuts),
        P(rows, None, None),
        P(rows, None, None),
        P(rows),
        P(rows),
        P(rows, None, None),
        P(rows),
        P(rows, None),
        P(rows),
        P(cuts, None),
    )
    return jax.shard_map(body, mesh=grid, in_specs=placed, out_specs=(P(rows, cuts), P(cuts, None)), check_vma=False)
```

```python
import functools

import jax
import jax.numpy as jnp
import numpy as np
from jax import lax
from jax.experimental import pallas as pl
from jax.experimental.pallas import tpu as pltpu
from jax.sharding import Mesh
from jax.sharding import PartitionSpec as P

CAP = 2

NX, NC, NY, NZ = 4, 2, 4, 8
PER = 11
HIGH = lax.Precision.HIGHEST


Z = ("zh", "zl")


def shifted(value, axis, distance):
    size = NZ if axis == Z else 4
    return lax.ppermute(value, axis, [(i, (i + distance) % size) for i in range(size)])


def crossing(k, back):
    pairs = []
    for x in range(NX):
        for z in range(NZ):
            half = (z % 2) ^ k
            there = (z // 2) * NZ + 2 * x + half
            pairs.append((there, x * NZ + z) if back else (x * NZ + z, there))
    return pairs


def crossed(first, second, odd, back):
    send = (jnp.where(odd, second, first), jnp.where(odd, first, second))
    got = [lax.ppermute(send[k], ("x", *Z), crossing(k, back)) for k in (0, 1)]
    return jnp.where(odd, got[1], got[0]), jnp.where(odd, got[0], got[1])


def product_kernel(tab, pa, pb, f0, x1, x2, x3, y1, y2, y3, own, ox1, ox2, ox3, oy1, oy2, oy3, fld, acc):
    for k, ref in enumerate((f0, x1, x2, x3, y1, y2, y3)):
        fld[16 * k : 16 * (k + 1)] = ref[...]
    acc[...] = jnp.zeros_like(acc)
    for part, ref in enumerate((pa, pb)):
        base = part * NZ * 2 * PER

        def step(q, carry, ref=ref, base=base):
            at = base + q * 2 * PER
            for first in range(0, PER, 2):
                places, terms = [], []
                for b in range(first, min(first + 2, PER)):
                    block = ref[q, b * 128 : (b + 1) * 128, :]
                    home = tab[at + b]
                    far = tab[at + PER + b]
                    places.append(home)
                    terms.append(
                        lax.dot_general(
                            fld[far], block, (((1,), (1,)), ((), ())), preferred_element_type=jnp.float32
                        )
                    )
                    if b < PER - 1:
                        places.append(far)
                        terms.append(
                            lax.dot_general(
                                fld[home], block, (((1,), (0,)), ((), ())), preferred_element_type=jnp.float32
                            )
                        )
                held = [acc[place] for place in places]
                for i, place in enumerate(places):
                    value = held[i]
                    for j in range(i):
                        value = jnp.where(places[j] == place, held[j], value)
                    held[i] = value + terms[i]
                for place, value in zip(places, held):
                    acc[place] = value
            return carry

        lax.fori_loop(0, NZ, step, 0)
    own[...] = acc[0:16]
    for k, ref in enumerate((ox1, ox2, ox3, oy1, oy2, oy3)):
        ref[...] = acc[16 * (k + 1) : 16 * (k + 2)].astype(jnp.bfloat16)


def products(tab, pa, pb, fields):
    cols = fields[0].shape[1]
    shape = (16, cols, 128)
    vmem = pl.BlockSpec(memory_space=pltpu.VMEM)
    return pl.pallas_call(
        product_kernel,
        out_shape=[jax.ShapeDtypeStruct(shape, jnp.float32)] + [jax.ShapeDtypeStruct(shape, jnp.bfloat16)] * 6,
        in_specs=[pl.BlockSpec(memory_space=pltpu.SMEM)] + [vmem] * 9,
        out_specs=[vmem] * 7,
        scratch_shapes=[
            pltpu.VMEM((112, cols, 128), jnp.bfloat16),
            pltpu.VMEM((112, cols, 128), jnp.float32),
        ],
        compiler_params=pltpu.CompilerParams(vmem_limit_bytes=40 << 20),
        cost_estimate=pl.CostEstimate(flops=336 * 2 * 64 * 128 * 128, bytes_accessed=8 << 20, transcendentals=0),
        name="products",
    )(tab, pa, pb, *fields)


def own_payload(diag_blocks, local_blocks, local_first, local_second, far_blocks, far_home, far_device, far_cluster):
    x, c, y, z = (lax.axis_index(a) for a in ("x", "core", "y", Z))
    target = far_device[:, 0]
    to_y, to_z = target // NZ, target % NZ
    pairs = far_blocks.shape[0]
    number = jnp.arange(pairs, dtype=jnp.int32)
    before = jnp.sum(
        ((target[None, :] == target[:, None]) & (number[None, :] < number[:, None])).astype(jnp.int32), axis=1
    )
    slot = (to_y % 2) * 4 + (to_z % 2) * CAP + before
    mine = (to_z // 2 == x) & (to_y // 2 == c)
    chosen = (slot[None, :] == jnp.arange(8, dtype=jnp.int32)[:, None]) & mine[None, :]
    taken = chosen.astype(jnp.int32)
    home_base = ((x - z // 2) % NX) * 16 + (z % 2) * 8
    away = (y - to_y) % NY
    far_index = jnp.where(away == 0, 0, 3 + away) * 16 + (to_z % 2) * 8 + far_cluster
    far_h = home_base + jnp.sum(taken * far_home[None, :], axis=1)
    far_f = jnp.sum(taken * far_index[None, :], axis=1)
    far_part = jnp.einsum(
        "sp,pab->sab", chosen.astype(jnp.bfloat16), far_blocks, preferred_element_type=jnp.float32
    ).astype(jnp.bfloat16)
    at = 4 * x + 2 * c
    local_part = lax.dynamic_slice_in_dim(local_blocks, at, 2, 0)
    loc_h = home_base + lax.dynamic_slice_in_dim(local_first, at, 2, 0)
    loc_f = home_base + lax.dynamic_slice_in_dim(local_second, at, 2, 0)
    raw = lax.dynamic_slice_in_dim(diag_blocks, 2 * x + c, 1, 0).astype(jnp.float32)
    diag_part = (0.5 * (raw + jnp.swapaxes(raw, 1, 2))).astype(jnp.bfloat16)
    dia = (home_base + 2 * x + c)[None]
    homes = jnp.concatenate([far_h, loc_h, dia])
    fars = jnp.concatenate([far_f, loc_f, dia])
    table = jnp.pad(jnp.stack([homes, fars]), ((0, 14), (0, 128 - PER))).astype(jnp.bfloat16)
    blocks = jnp.concatenate([far_part, local_part, diag_part]).reshape(PER * 128, 128)
    return jnp.concatenate([blocks, table])


def spread(payload, field, gathered):
    up = down = payload
    got = [payload]
    for n in range(3):
        up = shifted(up, Z, 1)
        down = shifted(down, Z, -1)
        got += [up, down]
        if n == 0:
            up, down, field = lax.optimization_barrier((up, down, field))
            fields = gathered(field)
        if n == 2:
            up, down, *fields = lax.optimization_barrier((up, down, *fields))
    cut = 704
    got.append(jnp.concatenate([shifted(up[:cut], Z, 1), shifted(down[cut:], Z, -1)]))
    mine = jnp.stack(got)
    other = lax.ppermute(mine, "core", [(0, 1), (1, 0)])
    return mine, other, fields


def table_of(payload):
    return payload[:, PER * 128 : PER * 128 + 2, :PER].astype(jnp.int32).reshape(-1)


def share_of(value):
    pieces = value.reshape(NY * NZ, -1, 128)
    pieces = lax.all_to_all(pieces, ("y", "x", "zl"), 0, 0, tiled=True)
    return jnp.sum(pieces.astype(jnp.float32), axis=0)


def put_together(share):
    every = jnp.broadcast_to(share[None], (NY * NZ, *share.shape))
    return lax.all_to_all(every, ("y", *Z), 0, 0, tiled=True).reshape(-1, 128)


def mm(a, b, contract=(1, 0)):
    dims = (((contract[0],), (contract[1],)), ((), ()))
    return lax.dot_general(a, b, dims, precision=HIGH, preferred_element_type=jnp.float32)


def inverse_factors(grams, srefs, erefs):
    row = lax.broadcasted_iota(jnp.int32, (128, 128), 0)
    col = lax.broadcasted_iota(jnp.int32, (128, 128), 1)
    eye = jnp.where(row == col, 1.0, 0.0).astype(jnp.float32)
    half_low = jnp.where(row > col, 1.0, 0.5 * eye)
    inverses, states = [], []
    for gram in grams:
        down = lax.rsqrt(jnp.sum(gram * eye, axis=1, keepdims=True))
        along = lax.rsqrt(jnp.sum(gram * eye, axis=0, keepdims=True))
        inverses.append(eye * down)
        states.append(gram * down * along)
    for _ in range(3):
        steps = [eye - half_low * (state - eye) for state in states]
        inverses = [mm(step, inverse) for step, inverse in zip(steps, inverses)]
        states = [mm(step, state) for step, state in zip(steps, states)]
        states = [mm(state, step, (1, 1)) for step, state in zip(steps, states)]
    states = [mm(inverse, gram) for inverse, gram in zip(inverses, grams)]
    states = [mm(state, inverse, (1, 1)) for inverse, state in zip(inverses, states)]
    for gram, inverse, state, sref, eref in zip(grams, inverses, states, srefs, erefs):
        eref[...] = mm(eye - half_low * (state - eye), inverse)
        close = jnp.max(jnp.abs(state - eye)) < 1e-3

        @pl.when(jnp.logical_not(close))
        def _(gram=gram, sref=sref, eref=eref):
            sref[...] = gram
            eref[...] = eye

            def step(k, carry):
                value = sref[...]
                top = sref[pl.ds(k, 1), :]
                pivot = jnp.sum(jnp.where(col[:1] == k, top, 0.0), axis=1, keepdims=True)
                left = jnp.sum(jnp.where(col == k, value, 0.0), axis=1, keepdims=True)
                scale = jnp.where(row[:, :1] > k, left / pivot, 0.0)
                below = eref[...] - scale * eref[pl.ds(k, 1), :]
                sref[...] = value - scale * top
                eref[...] = below
                return carry

            lax.fori_loop(0, 128, step, 0)
            eref[...] = eref[...] * lax.rsqrt(jnp.sum(sref[...] * eye, axis=1, keepdims=True))

    return [eref[...] for eref in erefs]


def joined(low, high):
    return jnp.concatenate([low, high], axis=0)


def inner(a, b):
    return lax.dot_general(a, b, (((1,), (1,)), ((), ())), preferred_element_type=jnp.float32)


def grams_kernel(v, t, y, low, out):
    sums = [jnp.zeros((128, 128), jnp.float32)] * 5
    for c in range(8):
        vc, tc, yc, lc = (joined(ref[0, c], ref[1, c]) for ref in (v, t, y, low))
        for i, (left, right) in enumerate(((vc, vc), (lc, vc), (yc, tc), (yc, yc), (lc, lc))):
            sums[i] += inner(left, right)
    for i in range(5):
        out[128 * i : 128 * (i + 1)] = sums[i].astype(jnp.bfloat16)


def in_two(value):
    high = value.astype(jnp.bfloat16)
    return high, (value - high.astype(jnp.float32)).astype(jnp.bfloat16)


def finish_kernel(count, lead, limits, sums, v_ref, low, subspace, rayleigh, *refs):
    srefs, erefs = refs[:2], refs[2:]
    part = 1.0 / count
    vv, lv, yt, yy, ll = (sums[128 * i : 128 * (i + 1)] for i in range(5))
    row = lax.broadcasted_iota(jnp.int32, (128, 128), 0)
    col = lax.broadcasted_iota(jnp.int32, (128, 128), 1)
    ll = jnp.where(lead[0] == 1, jnp.where(row == col, count, 0.0), ll)
    a1, a_low = inverse_factors([yy * part, ll * part], srefs, erefs)
    projection = mm(mm(a_low, lv), a1, (1, 1))
    whole = mm(mm(a1, vv), a1, (1, 1))
    deflated = whole - part * mm(projection, projection, (0, 0))
    (a2,) = inverse_factors([deflated * part], srefs[:1], erefs[:1])
    keep = in_two(mm(a1, a2, (0, 1)))
    drop = in_two(mm(a_low, mm(projection, a2, (1, 1)), (0, 0)) * (-part))
    for c in range(8):
        rows = jnp.zeros((128, 128), jnp.float32)
        for source, rights in ((v_ref, keep), (low, drop)):
            left = joined(source[0, c], source[1, c])
            for right in rights:
                rows += lax.dot_general(
                    left, right, (((0,), (0,)), ((), ())), preferred_element_type=jnp.float32
                )
        subspace[c * 128 : (c + 1) * 128] = rows
    center = 0.5 * (limits[0, 1] + limits[0, 0])
    half_width = 0.5 * (limits[0, 1] - limits[0, 0])
    rayleigh[...] = mm(mm(a1, half_width * yt + center * yy), a1, (1, 1)) * part


def body(
    start_states,
    diag_blocks,
    local_blocks,
    local_first,
    local_second,
    far_blocks,
    far_home,
    far_device,
    far_cluster,
    bounds,
):
    z = lax.axis_index(Z)
    odd = z % 2 == 1
    count = 1024.0 * NY * NZ
    turned = jnp.swapaxes(start_states.reshape(8, 128, 128), 1, 2).reshape(8, 2, 64, 128)
    field = jnp.concatenate(crossed(turned[:, 0], turned[:, 1], odd, False))
    limits = lax.ppermute(bounds, ("x", *Z), crossing(0, False))
    center = 0.5 * (limits[0, 1] + limits[0, 0])
    half_width = 0.5 * (limits[0, 1] - limits[0, 0])
    payload = own_payload(
        diag_blocks, local_blocks, local_first, local_second, far_blocks, far_home, far_device, far_cluster
    )

    def gathered(rounded):
        fields = [rounded]
        fields += [shifted(rounded, "x", k) for k in (1, 2, 3)]
        fields += [shifted(rounded, "y", k) for k in (1, 2, 3)]
        return fields

    pa, pb, fields = spread(payload, field, gathered)
    tab = jnp.concatenate([table_of(pa), table_of(pb)])

    def operate(fields):
        own, *sums = products(tab, pa, pb, fields)
        for k in (1, 2, 3):
            own = own + shifted(sums[k - 1], "x", -k).astype(jnp.float32)
            own = own + shifted(sums[k + 2], "y", -k).astype(jnp.float32)
        return own

    def filtered(start, fields):
        middle = (operate(fields) - center * start) / half_width
        return middle, gathered(middle.astype(jnp.bfloat16))

    def last(start, middle, fields):
        return 2.0 * (operate(fields) - center * middle) / half_width - start

    def paired(value):
        value = value.astype(jnp.bfloat16)
        low, high = value[:8], value[8:]
        got = lax.ppermute(jnp.where(odd, low, high), Z, [(i, i ^ 1) for i in range(NZ)])
        kept = jnp.where(odd, high, low)
        return jnp.stack([jnp.where(odd, got, kept), jnp.where(odd, kept, got)])

    def placed(value):
        return lax.ppermute(value, ("x", *Z), crossing(0, True))

    start = field.astype(jnp.float32)
    middle, fields = filtered(start, fields)
    first = last(start, middle, fields)
    fields = gathered(first.astype(jnp.bfloat16))
    y_rows, *fields = lax.optimization_barrier((paired(first), *fields))
    middle, fields = filtered(first, fields)
    below = [(z, NZ + z) for z in range(NZ)] + [(NZ + z, z + 2) for z in range(NZ - 2)]
    y_low = lax.ppermute(y_rows, ("core", *Z), below)
    t_rows, y_low, *fields = lax.optimization_barrier((paired(middle), y_low, *fields))
    y_placed = placed(y_low)
    second = last(first, middle, fields)
    v_rows = paired(second)
    v_placed = placed(v_rows)
    vmem = pl.BlockSpec(memory_space=pltpu.VMEM)
    smem = pl.BlockSpec(memory_space=pltpu.SMEM)
    sums = pl.pallas_call(
        grams_kernel,
        out_shape=jax.ShapeDtypeStruct((640, 128), jnp.bfloat16),
        in_specs=[vmem] * 4,
        out_specs=vmem,
        name="gram_sums",
    )(v_rows, t_rows, y_rows, y_low)
    share = placed(share_of(sums))
    sums = put_together(share)
    lead = ((lax.axis_index("x") == 0) & (lax.axis_index("core") == 0)).astype(jnp.int32)[None]
    subspace, rayleigh = pl.pallas_call(
        functools.partial(finish_kernel, count),
        out_shape=[jax.ShapeDtypeStruct((1024, 128), jnp.float32), jax.ShapeDtypeStruct((128, 128), jnp.float32)],
        in_specs=[smem, smem] + [vmem] * 3,
        out_specs=[vmem] * 2,
        scratch_shapes=[pltpu.VMEM((128, 128), jnp.float32)] * 4,
        name="finish",
    )(lead, bounds, sums, v_placed, y_placed)
    return subspace, rayleigh


def solution(mesh):
    grid = Mesh(np.asarray(mesh.devices).reshape(NX, NC, NY, NZ // 2, 2), ("x", "core", "y", *Z))
    rows, cuts = ("y", *Z), ("x", "core")
    placed = (
        P(rows, cuts),
        P(rows, None, None),
        P(rows, None, None),
        P(rows),
        P(rows),
        P(rows, None, None),
        P(rows),
        P(rows, None),
        P(rows),
        P(cuts, None),
    )
    return jax.shard_map(body, mesh=grid, in_specs=placed, out_specs=(P(rows, cuts), P(cuts, None)), check_vma=False)
```
